32 devices in a mesh: visit: 2 (over x), patch: 16 (over z, y, core).
Axes of the slice: x: 2, y: 2, z: 4, core: 2. Of those that a mesh axis runs over, the one named last changes fastest.
Arguments:
- images: bfloat16 [2, 96, 128, 512], P('visit', 'patch'), may hold values from -12 to 12
- coefficients: float32 [2, 96, 3, 40], P('visit', 'patch'), may hold values from -2 to 2
- intersection: int32 [2, 96, 2], P('visit'), may hold values from 0 to 15, as said below
- row_offset: int32 [2, 96], P('visit'), may hold values from 0 to 7
- col_offset: int32 [2, 96], P('visit'), may hold values from 0 to 511
- shifts: float32 [2, 96, 2], P('visit'), may hold values from 0 to 1
- inv_var: float32 [2, 96], P('visit'), may hold values from 0.3 to 3
Outputs:
- coadd: float32 [128, 8192], P('visit', 'patch')
- detection: float32 [128, 8192], P('visit', 'patch')
The draws below stay inside these ranges and needn't reach their ends.
Inputs may be any that keep to these rules, and one draw needn't show every extreme that they name: intersection[v, c, 1] = intersection[v, c, 0] + 1. Within each aligned block of 6 exposures of a visit (c from b * 6 to (b + 1) * 6 - 1), no patch is named twice.
All inputs are finite; a program needn't handle non-finite values.
Results may differ from the reference program's by a relative error of at most 0.0061.
Values may be sent and summed in bfloat16 or wider, within the bound.
No kernel may reach another device: no remote copies, remote signals or barrier semaphores. Data moves between devices by JAX's collectives and lax.ppermute only.
A program may use at most 128 MiB of HBM per device.

```python
import math
import jax
import jax.numpy as jnp
from jax import lax

CCD_DEV = 6
CH = 128
CW = 512
TERMS = 40
KRAD = 10
DITHER = 8
DRAD = 4
VISITS = 2
CCDS = 96
SKYW = 8192
N_PATCH = 16


def draw_intersection(key, part):
    stretch_extent = N_PATCH - CCD_DEV
    hot_width = max(stretch_extent // 4, 1)

    def one_device(visit, processor_unit):
        hot_key = jax.random.fold_in(key, 7000 + visit)
        hot_start = jax.random.randint(hot_key, (), 0, stretch_extent)
        device_key = jax.random.fold_in(key, visit * N_PATCH + processor_unit + 1)
        score_key, order_key = jax.random.split(device_key)
        baseline_level = jax.random.randint(score_key, (stretch_extent,), 0, 1024)
        free_positions = jnp.arange(stretch_extent)
        busy_region = (free_positions - hot_start) % stretch_extent < hot_width
        extra_credit = jnp.where((processor_unit == 0) & (free_positions == stretch_extent - 1), 2 << 14, 0) + jnp.where((processor_unit == 0) & (free_positions == 0), 1 << 14, 0)
        ranking_score = (baseline_level * jnp.where(busy_region, 2, 1) + extra_credit) * stretch_extent + free_positions
        picked = lax.top_k(ranking_score, CCD_DEV)[1]
        chosen = jnp.sort(picked)
        anchors = chosen + jnp.arange(CCD_DEV)
        anchors = jax.random.permutation(order_key, anchors)
        return jnp.stack([anchors, anchors + 1], -1)
    inner = jax.vmap(one_device, (None, 0))
    grid = jax.vmap(inner, (0, None))(jnp.arange(VISITS), jnp.arange(N_PATCH))
    return grid.reshape(VISITS, CCDS, 2).astype(jnp.int32)


def with_ends(array, rng, low, top_value):
    longest = array.shape.index(max(array.shape))
    spots = []
    for shift in (0, 1):
        where = [jax.random.randint(jax.random.fold_in(rng, axis), (), 0, length) for axis, length in enumerate(array.shape)]
        where[longest] = (where[longest] + shift) % array.shape[longest]
        spots.append(tuple(where))
    return array.at[spots[0]].set(low).at[spots[1]].set(top_value)


def steps_of(stream_key, shape, cuts, low, largest):
    def one(dim, shards_of):
        draws = jax.random.uniform(jax.random.fold_in(jax.random.fold_in(stream_key, 6), dim), (shards_of,), jnp.float32, low / len(cuts), largest / len(cuts))
        return jnp.repeat(jnp.exp(draws), shape[dim] // shards_of).reshape((-1,) + (1,) * (len(shape) - dim - 1))

    factor_of = one(*cuts[0])
    for cut in cuts[1:]:
        factor_of = factor_of * one(*cut)
    return factor_of


def scatter_about(stream_key, extent, width, limit, shards=(), dtype=jnp.bfloat16):
    values = jax.random.normal(stream_key, extent, jnp.float32) * width
    if len(shards) > 0:
        values = steps_of(stream_key, extent, shards, -0.22, 0.18) * values
    return jnp.clip(values, min=-limit, max=limit).astype(dtype)


def setup_inputs(seed: int = 0) -> dict:
    arg_keys = jax.random.split(jax.random.key(seed), 8)
    images = scatter_about(arg_keys[0], (VISITS, CCDS, CH, CW), 2.0, 12.0, ((0, 2), (1, 16)))
    coefficients = scatter_about(arg_keys[1], (VISITS, CCDS, 3, TERMS), 0.15, 2.0, ((0, 2), (1, 16)), jnp.float32)
    intersection = draw_intersection(jax.random.fold_in(arg_keys[7], 71), 0)
    row_offset = with_ends(jax.random.randint(arg_keys[3], (VISITS, CCDS), 0, DITHER), jax.random.fold_in(arg_keys[3], 1), 0, DITHER - 1).astype(jnp.int32)
    col_offset = with_ends(jax.random.randint(arg_keys[4], (VISITS, CCDS), 0, CW), jax.random.fold_in(arg_keys[4], 1), 0, CW - 1).astype(jnp.int32)
    shifts = jnp.clip(1.0 * jax.random.uniform(arg_keys[5], (VISITS, CCDS, 2), jnp.float32) ** steps_of(arg_keys[5], (VISITS, CCDS, 2), ((0, 2),), -0.2, 0.2), 0.0, 1.0)
    inv_var = jnp.clip(jnp.exp(math.log(3.0) - 2.3025851 * jax.random.uniform(arg_keys[6], (VISITS, CCDS), jnp.float32) ** steps_of(arg_keys[6], (VISITS, CCDS), ((0, 2),), -0.2, 0.2)), 0.3, 3.0)
    return {"images": images, "coefficients": coefficients, "intersection": intersection, "row_offset": row_offset, "col_offset": col_offset, "shifts": shifts, "inv_var": inv_var}


WIDTHS_PX = (1.0, 1.7, 2.6, 3.6)

def kernel_value(offsets, width_px, degree):
    scaled = offsets / width_px
    return scaled ** degree * jnp.exp(-offsets * offsets / (2.0 * width_px * width_px))

def basis_taps(radius):
    offsets = jnp.arange(-radius, radius + 1).astype(jnp.float32)
    profiles = []
    for group in range(4):
        for degree in range(4):
            profile = kernel_value(offsets, WIDTHS_PX[group], degree)
            profiles.append(profile / jnp.sqrt(jnp.sum(profile * profile)))
    return jnp.stack(profiles).reshape(4, 4, 2 * radius + 1).astype(jnp.bfloat16)

def match_exposure(exposure, weights, taps, row_pos, col_pos):
    radius = KRAD
    row_count, col_count = exposure.shape
    padded = jnp.pad(exposure.astype(jnp.float32), ((radius, radius), (0, 0)))
    smoothed = []
    for group in range(4):
        for y_degree in range(4):
            total = jnp.zeros((row_count, col_count), jnp.float32)
            for tap_idx in range(2 * radius + 1):
                total = total + taps[group, y_degree, tap_idx].astype(jnp.float32) * padded[tap_idx:tap_idx + row_count]
            smoothed.append(total.astype(jnp.bfloat16))
    matched = jnp.zeros((row_count, col_count), jnp.float32)
    term = 0
    for group in range(4):
        for x_degree in range(4):
            for y_degree in range(4 - x_degree):
                wide = jnp.pad(smoothed[group * 4 + y_degree].astype(jnp.float32), ((0, 0), (radius, radius)))
                response = jnp.zeros((row_count, col_count), jnp.float32)
                for tap_idx in range(2 * radius + 1):
                    response = response + taps[group, x_degree, tap_idx].astype(jnp.float32) * wide[:, tap_idx:tap_idx + col_count]
                factor = weights[0, term] + weights[1, term] * row_pos[:, None] + weights[2, term] * col_pos[None, :]
                matched = matched + factor * response
                term += 1
    return matched.astype(jnp.bfloat16)

def place_exposure(totals, exposure, anchor, row_shift, col_shift, frac_row, frac_col, weight):
    flux, cover = totals
    row_count, col_count = exposure.shape
    upper = lax.optimization_barrier((1.0 - frac_row).astype(jnp.bfloat16)).astype(jnp.float32)
    lower = lax.optimization_barrier(frac_row.astype(jnp.bfloat16)).astype(jnp.float32)
    left = lax.optimization_barrier((1.0 - frac_col).astype(jnp.bfloat16)).astype(jnp.float32)
    right = lax.optimization_barrier(frac_col.astype(jnp.bfloat16)).astype(jnp.float32)
    margin = DITHER + 1
    padded = jnp.pad(exposure.astype(jnp.float32), ((margin, 0), (0, 0)))
    zero = jnp.zeros((), jnp.int32)
    start_now = (margin - row_shift).astype(jnp.int32)
    current = lax.dynamic_slice(padded, (start_now, zero), (row_count, col_count))
    previous = lax.dynamic_slice(padded, (start_now - 1, zero), (row_count, col_count))
    middle = (upper * current + lower * previous).astype(jnp.bfloat16)
    wide = jnp.pad(middle.astype(jnp.float32), ((0, 0), (1, 1)))
    block = left * wide[:, 1:] + right * wide[:, :-1]
    row_index = jnp.arange(row_count).astype(jnp.int32)
    row_cover = upper * (row_index >= row_shift).astype(jnp.float32) + lower * (row_index >= row_shift + 1).astype(jnp.float32)
    col_index = jnp.arange(col_count + 1).astype(jnp.int32)
    col_cover = left * (col_index < col_count).astype(jnp.float32) + right * (col_index >= 1).astype(jnp.float32)
    column_start = (anchor * col_count + col_shift).astype(jnp.int32)
    old_flux = lax.dynamic_slice(flux, (zero, column_start), (row_count, col_count + 1))
    flux = lax.dynamic_update_slice(flux, old_flux + weight * block, (zero, column_start))
    old_cover = lax.dynamic_slice(cover, (zero, column_start), (row_count, col_count + 1))
    cover = lax.dynamic_update_slice(cover, old_cover + weight * row_cover[:, None] * col_cover[None, :], (zero, column_start))
    return (flux, cover)

def detect(framed, radius):
    offsets = jnp.arange(-radius, radius + 1).astype(jnp.float32)
    profile = jnp.exp(-offsets * offsets / 8.0)
    profile = profile / jnp.sqrt(jnp.sum(profile * profile))
    row_count = framed.shape[0] - 2 * radius
    col_count = framed.shape[1] - 2 * radius
    across = jnp.zeros((row_count, framed.shape[1]), jnp.float32)
    for tap_idx in range(2 * radius + 1):
        across = across + profile[tap_idx] * framed[tap_idx:tap_idx + row_count]
    result = jnp.zeros((row_count, col_count), jnp.float32)
    for tap_idx in range(2 * radius + 1):
        result = result + profile[tap_idx] * across[:, tap_idx:tap_idx + col_count]
    return result

def reference(images, coefficients, intersection, row_offset, col_offset, shifts, inv_var):
    taps = basis_taps(KRAD)
    row_pos = (2.0 * jnp.arange(CH).astype(jnp.float32) + 1.0) / CH - 1.0
    col_pos = (2.0 * jnp.arange(CW).astype(jnp.float32) + 1.0) / CW - 1.0
    flux = jnp.zeros((CH, SKYW), jnp.float32)
    cover = jnp.zeros((CH, SKYW), jnp.float32)
    for visit in range(VISITS):
        matched = lax.map(lambda operands: match_exposure(operands[0], operands[1], taps, row_pos, col_pos), (images[visit], coefficients[visit]))

        def add_one(ccd, totals):
            return place_exposure(totals, matched[ccd], intersection[visit, ccd, 0], row_offset[visit, ccd], col_offset[visit, ccd], shifts[visit, ccd, 0], shifts[visit, ccd, 1], inv_var[visit, ccd])
        flux, cover = lax.fori_loop(0, CCDS, add_one, (flux, cover))
    coadd = flux / jnp.maximum(cover, 1.0)
    framed = jnp.pad(coadd, DRAD)
    return (coadd, detect(framed, DRAD))
```

```python
import functools
import jax
import jax.numpy as jnp
import numpy as np
from jax import lax
from jax.experimental import pallas as pl
from jax.experimental.pallas import tpu as pltpu
from jax.sharding import PartitionSpec as P

KRAD = 10
DRAD = 4
WIDTHS_PX = (1.0, 1.7, 2.6, 3.6)
LANE = 128
PAIRS = [(s, d) for s in range(4) for d in range(4)]
CHUNKS = ((0, 3), (3, 6))
VMEM_LIMIT = 56 * 1024 * 1024


def basis_taps():
    t = np.arange(-KRAD, KRAD + 1).astype(np.float32)
    taps = []
    for s, d in PAIRS:
        w = np.float32(WIDTHS_PX[s])
        profile = (t / w) ** d * np.exp(-t * t / (np.float32(2.0) * w * w))
        taps.append(profile / np.sqrt(np.sum(profile * profile)))
    return np.stack(taps).astype(np.float32).astype(jnp.bfloat16)


def column_table(taps):
    window = np.arange(2 * LANE)[:, None]
    column = np.arange(LANE)[None, :]
    tap = window - LANE // 2 - column
    inside = np.abs(tap) <= KRAD
    index = np.clip(tap + KRAD, 0, 2 * KRAD)
    blocks = [np.where(inside, row[index], row.dtype.type(0)) for row in taps]
    return np.concatenate(blocks, axis=1)


def row_table(taps):
    row = np.arange(16)[:, None]
    lane = np.arange(LANE)[None, :]
    tap = (lane - row + LANE // 2) % LANE - LANE // 2
    inside = np.abs(tap) <= KRAD
    index = np.clip(tap + KRAD, 0, 2 * KRAD)
    return np.stack([np.where(inside, t[index], t.dtype.type(0)).astype(np.float32) for t in taps])


def iota(shape, dim):
    return lax.broadcasted_iota(jnp.int32, shape, dim)


class Plan:
    def __init__(self, mesh, height, width):
        self.visits = mesh.shape["visit"]
        self.patches = mesh.shape["patch"]
        self.height = height
        self.width = width
        self.block = height // self.visits
        if self.visits == 2:
            self.useful = self.block + DRAD
            self.step, self.first = self.block - DRAD, 0
        else:
            self.useful = self.block + 2 * DRAD
            self.step, self.first = self.block, -DRAD
        self.rows = -(-(self.useful + 4) // 8) * 8

    def base(self, visit):
        return visit * self.step + self.first


def match_kernel(plan, first, where_ref, row_ref, shift_ref, coef_ref, image_ref, table_ref, tap_ref, *rest):
    outs, (grid_ref, left_ref) = rest[:-2], rest[-2:]
    step = pl.program_id(0)
    ccd = first + step
    visit = where_ref[0]
    index = where_ref[1] * where_ref[2] + ccd
    height, width = plan.height, plan.width
    tiles = width // LANE

    image = image_ref[0, 0]
    edge = jnp.zeros((height, LANE // 2), image.dtype)
    padded = jnp.concatenate([edge, image, edge], axis=1)
    for pair in range(8):
        table = table_ref[:, pair * 256 : (pair + 1) * 256]
        for t in range(tiles):
            out = jnp.dot(padded[:, t * LANE : (t + 2) * LANE], table, preferred_element_type=jnp.float32)
            out = out.astype(jnp.bfloat16)
            for half in range(2):
                g = pair * 2 + half
                grid_ref[g * height : (g + 1) * height, t * LANE : (t + 1) * LANE] = out[:, half * LANE : (half + 1) * LANE]

    local_row = iota((16, LANE), 0).astype(jnp.float32)
    lane = iota((16, LANE), 1)
    yn = (2.0 * local_row + 1.0) / height - 1.0
    for g, (s, i) in enumerate(PAIRS):
        term = s * 10 + (0, 4, 7, 9)[i]
        sums = []
        for q in range(3):
            total = coef_ref[0, ccd, q, term] * tap_ref[s * 4]
            for j in range(1, 4 - i):
                total = total + coef_ref[0, ccd, q, term + j] * tap_ref[s * 4 + j]
            sums.append(total)
        steady = sums[0] + yn * sums[1]
        flat = sums[2].astype(jnp.bfloat16)
        for b in range(height // 16):
            tall = (steady + (32.0 * b / height) * sums[1]).astype(jnp.bfloat16)
            wide = flat
            if b:
                tall = pltpu.roll(tall, 16 * b, 1)
                wide = pltpu.roll(wide, 16 * b, 1)
            if b == 0:
                tall = jnp.where(lane < LANE // 2, tall, jnp.zeros_like(tall))
                wide = jnp.where(lane < LANE // 2, wide, jnp.zeros_like(wide))
            if b == height // 16 - 1:
                tall = jnp.where(lane >= LANE // 2, tall, jnp.zeros_like(tall))
                wide = jnp.where(lane >= LANE // 2, wide, jnp.zeros_like(wide))
            left_ref[16 * b : 16 * b + 16, g * LANE : (g + 1) * LANE] = tall
            left_ref[height + 16 * b : height + 16 * b + 16, g * LANE : (g + 1) * LANE] = wide

    both = jnp.dot(left_ref[...], grid_ref[...], preferred_element_type=jnp.float32)
    xn = (2.0 * iota((height, width), 1).astype(jnp.float32) + 1.0) / width - 1.0
    matched = (both[:height] + xn * both[height:]).astype(jnp.bfloat16)

    shift = row_ref[0, index]
    frac = jnp.full((plan.rows, height), shift_ref[0, index, 0], jnp.float32)
    upper = (1.0 - frac).astype(jnp.bfloat16)
    lower = frac.astype(jnp.bfloat16)
    local = iota((plan.rows, height), 0)
    source = iota((plan.rows, height), 1)
    nothing = jnp.zeros_like(upper)
    for d, out_ref in enumerate(outs):
        sky = local + plan.base(visit ^ d)
        good = (local < plan.useful) & (sky >= 0) & (sky < height)
        gap = jnp.where(good, source - sky + shift, 2 * height)
        rows = jnp.where(gap == 0, upper, jnp.where(gap == -1, lower, nothing))
        warped = jnp.dot(rows, matched, preferred_element_type=jnp.float32)
        out_ref[0] = warped.astype(jnp.bfloat16)


def match(plan, chunk, where, row_offset, shifts, coefficients, images, table, taps):
    first, last = chunk
    count = last - first
    smem = pl.BlockSpec(memory_space=pltpu.SMEM)
    height, width = plan.height, plan.width
    return pl.pallas_call(
        functools.partial(match_kernel, plan, first),
        name="match",
        grid=(count,),
        in_specs=[
            smem,
            smem,
            smem,
            smem,
            pl.BlockSpec((1, 1, height, width), lambda e: (0, first + e, 0, 0)),
            pl.BlockSpec(table.shape, lambda e: (0, 0)),
            pl.BlockSpec(taps.shape, lambda e: (0, 0, 0)),
        ],
        out_specs=[pl.BlockSpec((1, plan.rows, width), lambda e: (e, 0, 0))] * plan.visits,
        out_shape=[jax.ShapeDtypeStruct((count, plan.rows, width), jnp.bfloat16)] * plan.visits,
        scratch_shapes=[
            pltpu.VMEM((16 * height, width), jnp.bfloat16),
            pltpu.VMEM((2 * height, 16 * LANE), jnp.bfloat16),
        ],
        compiler_params=pltpu.CompilerParams(vmem_limit_bytes=VMEM_LIMIT),
    )(where, row_offset, shifts, coefficients, images, table, taps)


def place_kernel(plan, sizes, where_ref, *refs):
    metas = refs[: plan.visits]
    sources = refs[plan.visits : -3]
    send_ref, keep_ref, strip_ref = refs[-3:]
    rows, width = plan.rows, plan.width
    strip_ref[...] = jnp.zeros_like(strip_ref)
    gap = iota((2 * LANE, LANE), 0) - iota((2 * LANE, LANE), 1) - LANE
    nothing = jnp.zeros((2 * LANE, LANE), jnp.bfloat16)
    blank = jnp.zeros((rows, LANE), jnp.bfloat16)
    tiles = width // LANE
    spot = 0
    for first, last in sizes:
        for d in range(plan.visits):
            meta_ref, source_ref = metas[d], sources[spot]
            spot += 1
            for k in range(last - first):
                index = where_ref[1] * where_ref[2] + first + k
                start = meta_ref[index, 0].astype(jnp.int32)
                rem = start & (LANE - 1)
                tile = (start >> 7) + 1
                left = jnp.full(nothing.shape, meta_ref[index, 2], jnp.float32).astype(jnp.bfloat16)
                right = jnp.full(nothing.shape, meta_ref[index, 3], jnp.float32).astype(jnp.bfloat16)
                table = jnp.where(gap == -rem, left, jnp.where(gap == -rem - 1, right, nothing))
                source = jnp.concatenate([blank, source_ref[k], blank], axis=1)
                weight = meta_ref[index, 6]
                for t in range(tiles + 1):
                    out = jnp.dot(source[:, t * LANE : (t + 2) * LANE], table, preferred_element_type=jnp.float32)
                    strip_ref[tile + t] = strip_ref[tile + t] + weight * out

    core = where_ref[3] & 1
    chip = where_ref[3] >> 1
    pick = iota((8, LANE), 0) - 4
    lane = iota((8, LANE), 1)
    pick_left = ((pick >= 0) & (lane == LANE - 4 + pick)).astype(jnp.bfloat16)
    pick_right = ((pick >= 0) & (lane == pick)).astype(jnp.bfloat16)

    def across(table, block):
        out = lax.dot_general(table, block.astype(jnp.bfloat16), (((1,), (1,)), ((), ())), preferred_element_type=jnp.float32)
        return jnp.pad(out, ((0, 0), (0, LANE - rows)))

    def emit(m, parity, out_ref):
        tile = (2 * (chip ^ m) + parity) * tiles + 1
        sides = (across(pick_left, strip_ref[tile - 1]), across(pick_right, strip_ref[tile + tiles]))
        for t in range(tiles):
            body = strip_ref[tile + t]
            if t < 2:
                body = jnp.concatenate([body[: rows - 8], body[rows - 8 :] + sides[t]], axis=0)
            out_ref[m, :, t * LANE : (t + 1) * LANE] = body.astype(out_ref.dtype)

    for m in range(plan.patches // 2):
        emit(m, 1 - core, send_ref)
        emit(m, core, keep_ref)


def place(plan, sizes, where, metas, sources):
    smem = pl.BlockSpec(memory_space=pltpu.SMEM)
    vmem = pl.BlockSpec(memory_space=pltpu.VMEM)
    half = plan.patches // 2
    return pl.pallas_call(
        functools.partial(place_kernel, plan, sizes),
        name="place",
        in_specs=[smem] * (1 + plan.visits) + [vmem] * len(sources),
        out_specs=[vmem, vmem],
        out_shape=[
            jax.ShapeDtypeStruct((half, plan.rows, plan.width), jnp.bfloat16),
            jax.ShapeDtypeStruct((half, plan.rows, plan.width), jnp.float32),
        ],
        scratch_shapes=[pltpu.VMEM((plan.patches * plan.width // LANE + 2, plan.rows, LANE), jnp.float32)],
        compiler_params=pltpu.CompilerParams(vmem_limit_bytes=VMEM_LIMIT),
    )(where, *metas, *sources)


def fold_kernel(keep_ref, got_ref, *outs):
    for m, out_ref in enumerate(outs):
        out_ref[...] = (keep_ref[m] + got_ref[m].astype(jnp.float32)).astype(out_ref.dtype)


def fold(plan, keep, got):
    vmem = pl.BlockSpec(memory_space=pltpu.VMEM)
    half = plan.patches // 2
    shape = (plan.rows, plan.width)
    return pl.pallas_call(
        fold_kernel,
        name="fold",
        in_specs=[vmem, vmem],
        out_specs=[vmem] * half,
        out_shape=[jax.ShapeDtypeStruct(shape, jnp.float32)] + [jax.ShapeDtypeStruct(shape, jnp.bfloat16)] * (half - 1),
    )(keep, got)


def cover_kernel(plan, where_ref, *refs):
    metas, out_ref = refs[:-1], refs[-1]
    rows, width = plan.rows, plan.width
    column = where_ref[3] * width
    base = plan.base(where_ref[0])
    total = jnp.zeros((LANE, width), jnp.float32)
    sides = jnp.zeros((LANE, LANE), jnp.float32)
    for meta_ref in metas:
        meta = meta_ref[...]
        count = meta.shape[0]
        local = iota((count, LANE), 1)
        sky = (local + base).astype(jnp.float32)
        oy = meta[:, 1:2]
        rho = jnp.where(sky >= oy, meta[:, 4:5], 0.0) + jnp.where(sky >= oy + 1.0, meta[:, 5:6], 0.0)
        rho = jnp.where((local < plan.useful) & (sky >= 0) & (sky < plan.height), meta[:, 6:7] * rho, 0.0)

        def kappa(place):
            gap = place.astype(jnp.float32) - meta[:, 0:1]
            return jnp.where((gap >= 0) & (gap < width), meta[:, 2:3], 0.0) + jnp.where(
                (gap >= 1) & (gap < width + 1), meta[:, 3:4], 0.0
            )

        spot = iota((count, LANE), 1)
        side = jnp.where(spot < 8, spot - 8, spot - 12 + width)
        known = ((spot >= 4) & (spot < 8)) | ((spot >= 12) & (spot < 16))
        edge = jnp.where(known, kappa(side + column), 0.0)
        dims = (((0,), (0,)), ((), ()))
        kinds = dict(preferred_element_type=jnp.float32, precision=lax.Precision.HIGHEST)
        total = total + lax.dot_general(rho, kappa(iota((count, width), 1) + column), dims, **kinds)
        sides = sides + lax.dot_general(edge, rho, dims, **kinds)
    tail = total[rows - 8 : rows]
    tail = jnp.concatenate([tail[:, :LANE] + sides[:8], tail[:, LANE : 2 * LANE] + sides[8:16], tail[:, 2 * LANE :]], axis=1)
    out_ref[...] = jnp.concatenate([total[: rows - 8], tail], axis=0)


def cover_of(plan, where, metas):
    vmem = pl.BlockSpec(memory_space=pltpu.VMEM)
    return pl.pallas_call(
        functools.partial(cover_kernel, plan),
        name="cover",
        in_specs=[pl.BlockSpec(memory_space=pltpu.SMEM)] + [vmem] * plan.visits,
        out_specs=vmem,
        out_shape=jax.ShapeDtypeStruct((plan.rows, plan.width), jnp.float32),
    )(where, *metas)


def finish_kernel(plan, filt, where_ref, cover_ref, own_ref, *refs):
    parts, (coadd_ref, detect_ref) = refs[:-2], refs[-2:]
    rows, width, block = plan.rows, plan.width, plan.block
    flux = own_ref[...]
    for part in parts:
        flux = flux + part[...].astype(jnp.float32)
    coadd = flux / jnp.maximum(cover_ref[...], 1.0)
    visit = where_ref[0]
    if plan.step == block:
        coadd_ref[...] = coadd[-plan.first : -plan.first + block]
    else:
        coadd_ref[...] = jnp.where(visit == 0, coadd[:block], coadd[DRAD : DRAD + block])

    local = iota((block, LANE), 1)
    tap = local + plan.base(visit) - visit * block - iota((block, LANE), 0)
    good = (local < plan.useful) & (jnp.abs(tap) <= DRAD)
    band = jnp.zeros((block, LANE), jnp.float32)
    for t in range(-DRAD, DRAD + 1):
        band = jnp.where(good & (tap == t), filt[t + DRAD], band)
    kinds = dict(preferred_element_type=jnp.float32, precision=lax.Precision.HIGHEST)
    tall = jnp.concatenate([coadd, jnp.zeros((LANE - rows, width), jnp.float32)], axis=0)
    down = jnp.dot(band, tall, **kinds)
    blank = jnp.zeros((LANE - 8, LANE), jnp.float32)
    dims = (((1,), (1,)), ((), ()))
    before = lax.dot_general(band, jnp.concatenate([blank, coadd[rows - 8 :, :LANE]], axis=0), dims, **kinds)
    after = lax.dot_general(band, jnp.concatenate([coadd[rows - 8 :, LANE : 2 * LANE], blank], axis=0), dims, **kinds)
    lane = iota((block, LANE), 1)
    before = jnp.where(lane >= LANE - DRAD, before, 0.0)
    after = pltpu.roll(after, LANE - DRAD, 1)
    after = jnp.where(lane < DRAD, after, 0.0)
    wide = jnp.concatenate([before, down, after], axis=1)
    total = filt[DRAD] * wide
    for t in range(1, DRAD + 1):
        total = total + filt[DRAD + t] * (pltpu.roll(wide, t, 1) + pltpu.roll(wide, width + 2 * LANE - t, 1))
    detect_ref[...] = total[:, LANE : LANE + width]


def finish(plan, where, cover, own, parts):
    vmem = pl.BlockSpec(memory_space=pltpu.VMEM)
    t = np.arange(-DRAD, DRAD + 1).astype(np.float32)
    filt = np.exp(-t * t / np.float32(8.0))
    filt = filt / np.sqrt(np.sum(filt * filt))
    filt = [float(value) for value in filt]
    shape = jax.ShapeDtypeStruct((plan.block, plan.width), jnp.float32)
    return pl.pallas_call(
        functools.partial(finish_kernel, plan, filt),
        name="finish",
        in_specs=[pl.BlockSpec(memory_space=pltpu.SMEM)] + [vmem] * (2 + len(parts)),
        out_specs=[vmem, vmem],
        out_shape=[shape, shape],
    )(where, cover, own, *parts)


def narrow(value):
    return lax.reduce_precision(value, 8, 7)


def local(mesh, images, coefficients, intersection, row_offset, col_offset, shifts, inv_var):
    count, height, width = images.shape[1:]
    plan = Plan(mesh, height, width)
    taps = basis_taps()
    table, rows = jnp.asarray(column_table(taps)), jnp.asarray(row_table(taps))
    visit, patch = lax.axis_index("visit"), lax.axis_index("patch")
    where = jnp.stack([visit, patch, jnp.int32(count), patch]).astype(jnp.int32)
    frac_row, frac_col = shifts[0, :, 0:1], shifts[0, :, 1:2]
    start = intersection[0, :, 0:1] * width + col_offset[0][:, None]
    meta = jnp.concatenate(
        [
            start.astype(jnp.float32),
            row_offset[0][:, None].astype(jnp.float32),
            narrow(1.0 - frac_col),
            narrow(frac_col),
            narrow(1.0 - frac_row),
            narrow(frac_row),
            inv_var[0][:, None],
            jnp.zeros_like(frac_row),
        ],
        axis=1,
    )

    def swap(value, axis, bit):
        return lax.ppermute(value, axis, [(i, i ^ bit) for i in range(mesh.shape[axis])])

    metas = [meta] + [swap(meta, "visit", d) for d in range(1, plan.visits)]
    sources = []
    chunks = [(lo, min(hi, count)) for lo, hi in CHUNKS]
    for chunk in chunks:
        slots = match(plan, chunk, where, row_offset, shifts, coefficients, images, table, rows)
        sources += [slots[0]] + [swap(slots[d], "visit", d) for d in range(1, plan.visits)]
    cover = cover_of(plan, where, metas)
    send, keep = place(plan, chunks, where, metas, sources)
    folded = fold(plan, keep, swap(send, "patch", 1))
    parts = [swap(folded[m], "patch", 2 * m) for m in range(1, plan.patches // 2)]
    return finish(plan, where, cover, folded[0], parts)


def solution(mesh):
    return jax.shard_map(
        functools.partial(local, mesh),
        mesh=mesh,
        in_specs=(
            P("visit", "patch", None, None),
            P("visit", "patch", None, None),
            P("visit", None, None),
            P("visit", None),
            P("visit", None),
            P("visit", None, None),
            P("visit", None),
        ),
        out_specs=(P("visit", "patch"), P("visit", "patch")),
        check_vma=False,
    )
```

```python
import functools
import jax
import jax.numpy as jnp
import numpy as np
from jax import lax
from jax.experimental import pallas as pl
from jax.experimental.pallas import tpu as pltpu
from jax.sharding import PartitionSpec as P

KRAD = 10
DRAD = 4
WIDTHS_PX = (1.0, 1.7, 2.6, 3.6)
LANE = 128
PAIRS = [(s, d) for s in range(4) for d in range(4)]
CHUNKS = ((0, 3), (3, 6))
MIB = 1024 * 1024


def basis_taps():
    t = np.arange(-KRAD, KRAD + 1).astype(np.float32)
    taps = []
    for s, d in PAIRS:
        w = np.float32(WIDTHS_PX[s])
        profile = (t / w) ** d * np.exp(-t * t / (np.float32(2.0) * w * w))
        taps.append(profile / np.sqrt(np.sum(profile * profile)))
    return np.stack(taps).astype(np.float32).astype(jnp.bfloat16)


def column_table(taps):
    window = np.arange(2 * LANE)[:, None]
    column = np.arange(LANE)[None, :]
    tap = window - LANE // 2 - column
    inside = np.abs(tap) <= KRAD
    index = np.clip(tap + KRAD, 0, 2 * KRAD)
    blocks = [np.where(inside, row[index], row.dtype.type(0)) for row in taps]
    return np.concatenate(blocks, axis=1)


def row_table(taps):
    row = np.arange(16)[:, None]
    lane = np.arange(LANE)[None, :]
    tap = (lane - row + LANE // 2) % LANE - LANE // 2
    inside = np.abs(tap) <= KRAD
    index = np.clip(tap + KRAD, 0, 2 * KRAD)
    return np.stack([np.where(inside, t[index], t.dtype.type(0)).astype(np.float32) for t in taps])


def iota(shape, dim):
    return lax.broadcasted_iota(jnp.int32, shape, dim)


class Plan:
    def __init__(self, mesh, height, width):
        self.visits = mesh.shape["visit"]
        self.patches = mesh.shape["patch"]
        self.height = height
        self.width = width
        self.block = height // self.visits
        if self.visits == 2:
            self.useful = self.block + DRAD
            self.step, self.first = self.block - DRAD, 0
        else:
            self.useful = self.block + 2 * DRAD
            self.step, self.first = self.block, -DRAD
        self.rows = -(-(self.useful + 4) // 8) * 8

    def base(self, visit):
        return visit * self.step + self.first


def match_kernel(plan, first, total, row_ref, shift_ref, coef_ref, image_ref, table_ref, tap_ref, *rest):
    outs, (grid_ref, left_ref) = rest[:-2], rest[-2:]
    step = pl.program_id(0)
    ccd = first + step
    visit = lax.axis_index("visit")
    index = lax.axis_index("patch") * total + ccd
    height, width = plan.height, plan.width
    tiles = width // LANE

    image = image_ref[0, 0]
    edge = jnp.zeros((height, LANE // 2), image.dtype)
    padded = jnp.concatenate([edge, image, edge], axis=1)
    for pair in range(8):
        table = table_ref[:, pair * 256 : (pair + 1) * 256]
        for t in range(tiles):
            out = jnp.dot(padded[:, t * LANE : (t + 2) * LANE], table, preferred_element_type=jnp.float32)
            out = out.astype(jnp.bfloat16)
            for half in range(2):
                g = pair * 2 + half
                grid_ref[g * height : (g + 1) * height, t * LANE : (t + 1) * LANE] = out[:, half * LANE : (half + 1) * LANE]

    local_row = iota((16, LANE), 0).astype(jnp.float32)
    lane = iota((16, LANE), 1)
    yn = (2.0 * local_row + 1.0) / height - 1.0
    for g, (s, i) in enumerate(PAIRS):
        term = s * 10 + (0, 4, 7, 9)[i]
        sums = []
        for q in range(3):
            total = coef_ref[ccd, q, 0, term] * tap_ref[s * 4]
            for j in range(1, 4 - i):
                total = total + coef_ref[ccd, q, 0, term + j] * tap_ref[s * 4 + j]
            sums.append(total)
        steady = sums[0] + yn * sums[1]
        flat = sums[2].astype(jnp.bfloat16)
        for b in range(height // 16):
            tall = (steady + (32.0 * b / height) * sums[1]).astype(jnp.bfloat16)
            wide = flat
            if b:
                tall = pltpu.roll(tall, 16 * b, 1)
                wide = pltpu.roll(wide, 16 * b, 1)
            if b == 0:
                tall = jnp.where(lane < LANE // 2, tall, jnp.zeros_like(tall))
                wide = jnp.where(lane < LANE // 2, wide, jnp.zeros_like(wide))
            if b == height // 16 - 1:
                tall = jnp.where(lane >= LANE // 2, tall, jnp.zeros_like(tall))
                wide = jnp.where(lane >= LANE // 2, wide, jnp.zeros_like(wide))
            left_ref[16 * b : 16 * b + 16, g * LANE : (g + 1) * LANE] = tall
            left_ref[height + 16 * b : height + 16 * b + 16, g * LANE : (g + 1) * LANE] = wide

    both = jnp.dot(left_ref[...], grid_ref[...], preferred_element_type=jnp.float32)
    xn = (2.0 * iota((height, width), 1).astype(jnp.float32) + 1.0) / width - 1.0
    matched = (both[:height] + xn * both[height:]).astype(jnp.bfloat16)

    shift = row_ref[0, index]
    frac = jnp.full((plan.rows, height), shift_ref[0, 0, index], jnp.float32)
    upper = (1.0 - frac).astype(jnp.bfloat16)
    lower = frac.astype(jnp.bfloat16)
    local = iota((plan.rows, height), 0)
    source = iota((plan.rows, height), 1)
    nothing = jnp.zeros_like(upper)
    for d, out_ref in enumerate(outs):
        sky = local + plan.base(visit ^ d)
        good = (local < plan.useful) & (sky >= 0) & (sky < height)
        gap = jnp.where(good, source - sky + shift, 2 * height)
        rows = jnp.where(gap == 0, upper, jnp.where(gap == -1, lower, nothing))
        warped = jnp.dot(rows, matched, preferred_element_type=jnp.float32)
        out_ref[0] = warped.astype(jnp.bfloat16)


def match(plan, chunk, row_offset, shifts, coefficients, images, table, taps):
    first, last = chunk
    count = last - first
    smem = pl.BlockSpec(memory_space=pltpu.SMEM)
    height, width = plan.height, plan.width
    return pl.pallas_call(
        functools.partial(match_kernel, plan, first, images.shape[1]),
        name="match",
        grid=(count,),
        in_specs=[
            smem,
            smem,
            smem,
            pl.BlockSpec((1, 1, height, width), lambda e: (0, first + e, 0, 0)),
            pl.BlockSpec(table.shape, lambda e: (0, 0)),
            pl.BlockSpec(taps.shape, lambda e: (0, 0, 0)),
        ],
        out_specs=[pl.BlockSpec((1, plan.rows, width), lambda e: (e, 0, 0))] * plan.visits,
        out_shape=[jax.ShapeDtypeStruct((count, plan.rows, width), jnp.bfloat16)] * plan.visits,
        scratch_shapes=[
            pltpu.VMEM((16 * height, width), jnp.bfloat16),
            pltpu.VMEM((2 * height, 16 * LANE), jnp.bfloat16),
        ],
        compiler_params=pltpu.CompilerParams(vmem_limit_bytes=20 * MIB),
    )(row_offset, shifts, coefficients, images, table, taps)


def place_kernel(plan, sizes, total, *refs):
    metas = refs[: plan.visits]
    sources = refs[plan.visits : -3]
    send_ref, keep_ref, strip_ref = refs[-3:]
    rows, width = plan.rows, plan.width
    patch = lax.axis_index("patch")
    strip_ref[...] = jnp.zeros_like(strip_ref)
    gap = iota((2 * LANE, LANE), 0) - iota((2 * LANE, LANE), 1) - LANE
    nothing = jnp.zeros((2 * LANE, LANE), jnp.bfloat16)
    blank = jnp.zeros((rows, LANE), jnp.bfloat16)
    tiles = width // LANE
    spot = 0
    for first, last in sizes:
        for d in range(plan.visits):
            meta_ref, source_ref = metas[d], sources[spot]
            spot += 1
            for k in range(last - first):
                index = patch * total + first + k
                start = meta_ref[index, 0].astype(jnp.int32)
                rem = start & (LANE - 1)
                tile = (start >> 7) + 1
                left = jnp.full(nothing.shape, meta_ref[index, 2], jnp.float32).astype(jnp.bfloat16)
                right = jnp.full(nothing.shape, meta_ref[index, 3], jnp.float32).astype(jnp.bfloat16)
                table = jnp.where(gap == -rem, left, jnp.where(gap == -rem - 1, right, nothing))
                source = jnp.concatenate([blank, source_ref[k], blank], axis=1)
                weight = meta_ref[index, 6]
                for t in range(tiles + 1):
                    out = jnp.dot(source[:, t * LANE : (t + 2) * LANE], table, preferred_element_type=jnp.float32)
                    strip_ref[tile + t] = strip_ref[tile + t] + weight * out

    core = patch & 1
    chip = patch >> 1
    pick = iota((8, LANE), 0) - 4
    lane = iota((8, LANE), 1)
    pick_left = ((pick >= 0) & (lane == LANE - 4 + pick)).astype(jnp.bfloat16)
    pick_right = ((pick >= 0) & (lane == pick)).astype(jnp.bfloat16)

    def across(table, block):
        out = lax.dot_general(table, block.astype(jnp.bfloat16), (((1,), (1,)), ((), ())), preferred_element_type=jnp.float32)
        return jnp.pad(out, ((0, 0), (0, LANE - rows)))

    def emit(m, parity, out_ref):
        tile = (2 * (chip ^ m) + parity) * tiles + 1
        sides = (across(pick_left, strip_ref[tile - 1]), across(pick_right, strip_ref[tile + tiles]))
        for t in range(tiles):
            body = strip_ref[tile + t]
            if t < 2:
                body = jnp.concatenate([body[: rows - 8], body[rows - 8 :] + sides[t]], axis=0)
            out_ref[m, :, t * LANE : (t + 1) * LANE] = body.astype(out_ref.dtype)

    for m in range(plan.patches // 2):
        emit(m, 1 - core, send_ref)
        emit(m, core, keep_ref)


def place(plan, sizes, total, metas, sources):
    smem = pl.BlockSpec(memory_space=pltpu.SMEM)
    vmem = pl.BlockSpec(memory_space=pltpu.VMEM)
    half = plan.patches // 2
    return pl.pallas_call(
        functools.partial(place_kernel, plan, sizes, total),
        name="place",
        in_specs=[smem] * plan.visits + [vmem] * len(sources),
        out_specs=[vmem, vmem],
        out_shape=[
            jax.ShapeDtypeStruct((half, plan.rows, plan.width), jnp.bfloat16),
            jax.ShapeDtypeStruct((half, plan.rows, plan.width), jnp.float32),
        ],
        scratch_shapes=[pltpu.VMEM((plan.patches * plan.width // LANE + 2, plan.rows, LANE), jnp.float32)],
        compiler_params=pltpu.CompilerParams(vmem_limit_bytes=16 * MIB),
    )(*metas, *sources)


def fold_kernel(keep_ref, got_ref, *outs):
    for m, out_ref in enumerate(outs):
        out_ref[...] = (keep_ref[m] + got_ref[m].astype(jnp.float32)).astype(out_ref.dtype)


def fold(plan, keep, got):
    vmem = pl.BlockSpec(memory_space=pltpu.VMEM)
    half = plan.patches // 2
    shape = (plan.rows, plan.width)
    return pl.pallas_call(
        fold_kernel,
        name="fold",
        in_specs=[vmem, vmem],
        out_specs=[vmem] * half,
        out_shape=[jax.ShapeDtypeStruct(shape, jnp.float32)] + [jax.ShapeDtypeStruct(shape, jnp.bfloat16)] * (half - 1),
        compiler_params=pltpu.CompilerParams(vmem_limit_bytes=10 * MIB),
    )(keep, got)


def cover_kernel(plan, *refs):
    metas, out_ref = refs[:-1], refs[-1]
    rows, width = plan.rows, plan.width
    column = lax.axis_index("patch") * width
    base = plan.base(lax.axis_index("visit"))
    total = jnp.zeros((LANE, width), jnp.float32)
    sides = jnp.zeros((LANE, LANE), jnp.float32)
    for meta_ref in metas:
        meta = meta_ref[...]
        count = meta.shape[0]
        local = iota((count, LANE), 1)
        sky = (local + base).astype(jnp.float32)
        oy = meta[:, 1:2]
        rho = jnp.where(sky >= oy, meta[:, 4:5], 0.0) + jnp.where(sky >= oy + 1.0, meta[:, 5:6], 0.0)
        rho = jnp.where((local < plan.useful) & (sky >= 0) & (sky < plan.height), meta[:, 6:7] * rho, 0.0)

        def kappa(place):
            gap = place.astype(jnp.float32) - meta[:, 0:1]
            return jnp.where((gap >= 0) & (gap < width), meta[:, 2:3], 0.0) + jnp.where(
                (gap >= 1) & (gap < width + 1), meta[:, 3:4], 0.0
            )

        spot = iota((count, LANE), 1)
        side = jnp.where(spot < 8, spot - 8, spot - 12 + width)
        known = ((spot >= 4) & (spot < 8)) | ((spot >= 12) & (spot < 16))
        edge = jnp.where(known, kappa(side + column), 0.0)
        dims = (((0,), (0,)), ((), ()))
        kinds = dict(preferred_element_type=jnp.float32, precision=lax.Precision.HIGHEST)
        total = total + lax.dot_general(rho, kappa(iota((count, width), 1) + column), dims, **kinds)
        sides = sides + lax.dot_general(edge, rho, dims, **kinds)
    tail = total[rows - 8 : rows]
    tail = jnp.concatenate([tail[:, :LANE] + sides[:8], tail[:, LANE : 2 * LANE] + sides[8:16], tail[:, 2 * LANE :]], axis=1)
    out_ref[...] = jnp.concatenate([total[: rows - 8], tail], axis=0)


def cover_of(plan, metas):
    vmem = pl.BlockSpec(memory_space=pltpu.VMEM)
    return pl.pallas_call(
        functools.partial(cover_kernel, plan),
        name="cover",
        in_specs=[vmem] * plan.visits,
        out_specs=vmem,
        out_shape=jax.ShapeDtypeStruct((plan.rows, plan.width), jnp.float32),
        compiler_params=pltpu.CompilerParams(vmem_limit_bytes=10 * MIB),
    )(*metas)


def finish_kernel(plan, filt, cover_ref, own_ref, *refs):
    parts, (coadd_ref, detect_ref) = refs[:-2], refs[-2:]
    rows, width, block = plan.rows, plan.width, plan.block
    flux = own_ref[...]
    for part in parts:
        flux = flux + part[...].astype(jnp.float32)
    coadd = flux / jnp.maximum(cover_ref[...], 1.0)
    visit = lax.axis_index("visit")
    if plan.step == block:
        coadd_ref[...] = coadd[-plan.first : -plan.first + block]
    else:
        coadd_ref[...] = jnp.where(visit == 0, coadd[:block], coadd[DRAD : DRAD + block])

    local = iota((block, LANE), 1)
    tap = local + plan.base(visit) - visit * block - iota((block, LANE), 0)
    good = (local < plan.useful) & (jnp.abs(tap) <= DRAD)
    band = jnp.zeros((block, LANE), jnp.float32)
    for t in range(-DRAD, DRAD + 1):
        band = jnp.where(good & (tap == t), filt[t + DRAD], band)
    kinds = dict(preferred_element_type=jnp.float32, precision=lax.Precision.HIGHEST)
    tall = jnp.concatenate([coadd, jnp.zeros((LANE - rows, width), jnp.float32)], axis=0)
    down = jnp.dot(band, tall, **kinds)
    blank = jnp.zeros((LANE - 8, LANE), jnp.float32)
    dims = (((1,), (1,)), ((), ()))
    before = lax.dot_general(band, jnp.concatenate([blank, coadd[rows - 8 :, :LANE]], axis=0), dims, **kinds)
    after = lax.dot_general(band, jnp.concatenate([coadd[rows - 8 :, LANE : 2 * LANE], blank], axis=0), dims, **kinds)
    lane = iota((block, LANE), 1)
    before = jnp.where(lane >= LANE - DRAD, before, 0.0)
    after = pltpu.roll(after, LANE - DRAD, 1)
    after = jnp.where(lane < DRAD, after, 0.0)
    wide = jnp.concatenate([before, down, after], axis=1)
    total = filt[DRAD] * wide
    for t in range(1, DRAD + 1):
        total = total + filt[DRAD + t] * (pltpu.roll(wide, t, 1) + pltpu.roll(wide, width + 2 * LANE - t, 1))
    detect_ref[...] = total[:, LANE : LANE + width]


def finish(plan, cover, own, parts):
    vmem = pl.BlockSpec(memory_space=pltpu.VMEM)
    t = np.arange(-DRAD, DRAD + 1).astype(np.float32)
    filt = np.exp(-t * t / np.float32(8.0))
    filt = filt / np.sqrt(np.sum(filt * filt))
    filt = [float(value) for value in filt]
    shape = jax.ShapeDtypeStruct((plan.block, plan.width), jnp.float32)
    return pl.pallas_call(
        functools.partial(finish_kernel, plan, filt),
        name="finish",
        in_specs=[vmem] * (2 + len(parts)),
        out_specs=[vmem, vmem],
        out_shape=[shape, shape],
        compiler_params=pltpu.CompilerParams(vmem_limit_bytes=10 * MIB),
    )(cover, own, *parts)


def narrow(value):
    return lax.reduce_precision(value, 8, 7)


def local(mesh, images, coefficients, intersection, row_offset, col_offset, shifts, inv_var):
    count, height, width = images.shape[1:]
    plan = Plan(mesh, height, width)
    taps = basis_taps()
    table, rows = jnp.asarray(column_table(taps)), jnp.asarray(row_table(taps))
    frac_row, frac_col = shifts[0, :, 0:1], shifts[0, :, 1:2]
    start = intersection[0, :, 0:1] * width + col_offset[0][:, None]
    meta = jnp.concatenate(
        [
            start.astype(jnp.float32),
            row_offset[0][:, None].astype(jnp.float32),
            narrow(1.0 - frac_col),
            narrow(frac_col),
            narrow(1.0 - frac_row),
            narrow(frac_row),
            inv_var[0][:, None],
            jnp.zeros_like(frac_row),
        ],
        axis=1,
    )

    sides, factors = jnp.transpose(shifts, (0, 2, 1)), jnp.transpose(coefficients, (1, 2, 0, 3))

    def swap(value, axis, bit):
        return lax.ppermute(value, axis, [(i, i ^ bit) for i in range(mesh.shape[axis])])

    metas = [meta] + [swap(meta, "visit", d) for d in range(1, plan.visits)]
    sources = []
    chunks = [(lo, min(hi, count)) for lo, hi in CHUNKS]
    for chunk in chunks:
        slots = match(plan, chunk, row_offset, sides, factors, images, table, rows)
        sources += [slots[0]] + [swap(slots[d], "visit", d) for d in range(1, plan.visits)]
    cover = cover_of(plan, metas)
    send, keep = place(plan, chunks, count, metas, sources)
    folded = fold(plan, keep, swap(send, "patch", 1))
    parts = [swap(folded[m], "patch", 2 * m) for m in range(1, plan.patches // 2)]
    return finish(plan, cover, folded[0], parts)


def solution(mesh):
    return jax.shard_map(
        functools.partial(local, mesh),
        mesh=mesh,
        in_specs=(
            P("visit", "patch", None, None),
            P("visit", "patch", None, None),
            P("visit", None, None),
            P("visit", None),
            P("visit", None),
            P("visit", None, None),
            P("visit", None),
        ),
        out_specs=(P("visit", "patch"), P("visit", "patch")),
        check_vma=False,
    )
```

```python
import functools
import jax
import jax.numpy as jnp
import numpy as np
from jax import lax
from jax.experimental import pallas as pl
from jax.experimental.pallas import tpu as pltpu
from jax.sharding import PartitionSpec as P

KRAD = 10
DRAD = 4
WIDTHS_PX = (1.0, 1.7, 2.6, 3.6)
LANE = 128
PAIRS = [(s, d) for s in range(4) for d in range(4)]
CHUNKS = ((0, 3), (3, 6))
MIB = 1024 * 1024


def basis_taps():
    t = np.arange(-KRAD, KRAD + 1).astype(np.float32)
    taps = []
    for s, d in PAIRS:
        w = np.float32(WIDTHS_PX[s])
        profile = (t / w) ** d * np.exp(-t * t / (np.float32(2.0) * w * w))
        taps.append(profile / np.sqrt(np.sum(profile * profile)))
    return np.stack(taps).astype(np.float32).astype(jnp.bfloat16)


def column_table(taps):
    window = np.arange(2 * LANE)[:, None]
    column = np.arange(LANE)[None, :]
    tap = window - LANE // 2 - column
    inside = np.abs(tap) <= KRAD
    index = np.clip(tap + KRAD, 0, 2 * KRAD)
    blocks = [np.where(inside, row[index], row.dtype.type(0)) for row in taps]
    return np.concatenate(blocks, axis=1)


def row_table(taps):
    row = np.arange(16)[:, None]
    lane = np.arange(LANE)[None, :]
    tap = (lane - row + LANE // 2) % LANE - LANE // 2
    inside = np.abs(tap) <= KRAD
    index = np.clip(tap + KRAD, 0, 2 * KRAD)
    return np.stack([np.where(inside, t[index], t.dtype.type(0)).astype(np.float32) for t in taps])


def iota(shape, dim):
    return lax.broadcasted_iota(jnp.int32, shape, dim)


class Plan:
    def __init__(self, mesh, height, width):
        self.visits = mesh.shape["visit"]
        self.patches = mesh.shape["patch"]
        self.height = height
        self.width = width
        self.block = height // self.visits
        if self.visits == 2:
            self.useful = self.block + DRAD
            self.step, self.first = self.block - DRAD, 0
        else:
            self.useful = self.block + 2 * DRAD
            self.step, self.first = self.block, -DRAD
        self.rows = -(-(self.useful + 4) // 8) * 8
        self.near = self.patches // 4

    def base(self, visit):
        return visit * self.step + self.first


def match_kernel(plan, first, total, fetch, *refs):
    ins, rest = refs[:6], refs[6:]
    outs, rest = rest[: plan.visits], rest[plan.visits :]
    window_ref, grid_ref, left_ref = rest[:3]
    height, width = plan.height, plan.width
    tiles = width // LANE
    count = outs[0].shape[0]
    if fetch:
        homes, sems = rest[3:9], rest[9]
        copies = []
        for n in (2, 5, 3, 4, 0, 1):
            source = ins[n].at[:, pl.ds(first, count)] if n == 3 else ins[n]
            copies.append((n, pltpu.make_async_copy(source, homes[n], sems.at[n])))
        for n, copy in copies:
            copy.start()
        ins, base = homes, 0
        arrive = {n: copy.wait for n, copy in copies}
    else:
        base = first
        arrive = {n: lambda: None for n in range(6)}
    row_ref, shift_ref, coef_ref, image_ref, table_ref, tap_ref = ins

    arrive[2]()
    arrive[5]()
    local_row = iota((16, LANE), 0).astype(jnp.float32)
    lane = iota((16, LANE), 1)
    yn = (2.0 * local_row + 1.0) / height - 1.0

    def coefficients(e):
        for g, (s, i) in enumerate(PAIRS):
            term = s * 10 + (0, 4, 7, 9)[i]
            sums = []
            for q in range(3):
                total_tap = coef_ref[first + e, q, 0, term] * tap_ref[s * 4]
                for j in range(1, 4 - i):
                    total_tap = total_tap + coef_ref[first + e, q, 0, term + j] * tap_ref[s * 4 + j]
                sums.append(total_tap)
            steady = sums[0] + yn * sums[1]
            flat = sums[2].astype(jnp.bfloat16)
            for b in range(height // 16):
                tall = (steady + (32.0 * b / height) * sums[1]).astype(jnp.bfloat16)
                wide = flat
                if b:
                    tall = pltpu.roll(tall, 16 * b, 1)
                    wide = pltpu.roll(wide, 16 * b, 1)
                if b == 0:
                    tall = jnp.where(lane < LANE // 2, tall, jnp.zeros_like(tall))
                    wide = jnp.where(lane < LANE // 2, wide, jnp.zeros_like(wide))
                if b == height // 16 - 1:
                    tall = jnp.where(lane >= LANE // 2, tall, jnp.zeros_like(tall))
                    wide = jnp.where(lane >= LANE // 2, wide, jnp.zeros_like(wide))
                left_ref[e, 16 * b : 16 * b + 16, g * LANE : (g + 1) * LANE] = tall
                left_ref[e, height + 16 * b : height + 16 * b + 16, g * LANE : (g + 1) * LANE] = wide

    coefficients(0)
    arrive[3]()
    edge = jnp.zeros((height, LANE // 2), jnp.bfloat16)
    for e in range(count):
        padded = jnp.concatenate([edge, image_ref[0, base + e], edge], axis=1)
        for t in range(tiles):
            spot = (e * tiles + t) * height
            window_ref[spot : spot + height] = padded[:, t * LANE : (t + 2) * LANE]
    arrive[4]()
    for pair in range(8):
        out = jnp.dot(window_ref[...], table_ref[:, pair * 256 : (pair + 1) * 256], preferred_element_type=jnp.float32)
        out = out.astype(jnp.bfloat16)
        for e in range(count):
            for t in range(tiles):
                spot = (e * tiles + t) * height
                for half in range(2):
                    g = pair * 2 + half
                    grid_ref[e, g * height : (g + 1) * height, t * LANE : (t + 1) * LANE] = out[
                        spot : spot + height, half * LANE : (half + 1) * LANE
                    ]
    for e in range(1, count):
        coefficients(e)
    arrive[0]()
    arrive[1]()
    visit = lax.axis_index("visit")
    local = iota((plan.rows, height), 0)
    source = iota((plan.rows, height), 1)
    xn = (2.0 * iota((height, width), 1).astype(jnp.float32) + 1.0) / width - 1.0
    for e in range(count):
        index = lax.axis_index("patch") * total + first + e
        both = jnp.dot(left_ref[e], grid_ref[e], preferred_element_type=jnp.float32)
        matched = (both[:height] + xn * both[height:]).astype(jnp.bfloat16)
        shift = row_ref[0, index]
        frac = jnp.full((plan.rows, height), shift_ref[0, 0, index], jnp.float32)
        upper = (1.0 - frac).astype(jnp.bfloat16)
        lower = frac.astype(jnp.bfloat16)
        nothing = jnp.zeros_like(upper)
        for d, out_ref in enumerate(outs):
            sky = local + plan.base(visit ^ d)
            good = (local < plan.useful) & (sky >= 0) & (sky < height)
            gap = jnp.where(good, source - sky + shift, 2 * height)
            rows = jnp.where(gap == 0, upper, jnp.where(gap == -1, lower, nothing))
            warped = jnp.dot(rows, matched, preferred_element_type=jnp.float32)
            out_ref[e] = warped.astype(jnp.bfloat16)


def match(plan, chunk, fetch, row_offset, shifts, coefficients, images, table, taps):
    first, last = chunk
    count = last - first
    height, width = plan.height, plan.width
    operands = (row_offset, shifts, coefficients, images, table, taps)
    spaces = [pltpu.SMEM] * 3 + [pltpu.VMEM] * 3
    scratch = [
        pltpu.VMEM((count * 4 * height, 2 * LANE), jnp.bfloat16),
        pltpu.VMEM((count, 16 * height, width), jnp.bfloat16),
        pltpu.VMEM((count, 2 * height, 16 * LANE), jnp.bfloat16),
    ]
    if fetch:
        for n, (operand, space) in enumerate(zip(operands, spaces)):
            shape = (1, count) + operand.shape[2:] if n == 3 else operand.shape
            scratch.append(space(shape, operand.dtype))
        scratch.append(pltpu.SemaphoreType.DMA((6,)))
        spaces = [pltpu.HBM] * 6
    return pl.pallas_call(
        functools.partial(match_kernel, plan, first, images.shape[1], fetch),
        name="match",
        in_specs=[pl.BlockSpec(memory_space=space) for space in spaces],
        out_specs=[pl.BlockSpec(memory_space=pltpu.VMEM)] * plan.visits,
        out_shape=[jax.ShapeDtypeStruct((count, plan.rows, width), jnp.bfloat16)] * plan.visits,
        scratch_shapes=scratch,
        compiler_params=pltpu.CompilerParams(vmem_limit_bytes=61 * MIB),
    )(*operands)


def place_one(plan, strip_ref, gap, meta_ref, index, source):
    rows, width = plan.rows, plan.width
    tiles = width // LANE
    blank = jnp.zeros((rows, LANE), jnp.bfloat16)
    nothing = jnp.zeros(gap.shape, jnp.bfloat16)
    start = meta_ref[index, 0].astype(jnp.int32)
    rem = start & (LANE - 1)
    tile = (start >> 7) + 1
    left = jnp.full(gap.shape, meta_ref[index, 2], jnp.float32).astype(jnp.bfloat16)
    right = jnp.full(gap.shape, meta_ref[index, 3], jnp.float32).astype(jnp.bfloat16)
    table = jnp.where(gap == -rem, left, jnp.where(gap == -rem - 1, right, nothing))
    source = jnp.concatenate([blank, source, blank], axis=1)
    windows = jnp.concatenate([source[:, t * LANE : (t + 2) * LANE] for t in range(tiles + 1)], axis=0)
    out = jnp.dot(windows, table, preferred_element_type=jnp.float32)
    weight = meta_ref[index, 6]
    for t in range(tiles + 1):
        strip_ref[tile + t] = strip_ref[tile + t] + weight * out[t * rows : (t + 1) * rows]


def place_all(plan, strip_ref, total, metas, jobs, sources):
    patch = lax.axis_index("patch")
    gap = iota((2 * LANE, LANE), 0) - iota((2 * LANE, LANE), 1) - LANE
    for (d, first, last), source_ref in zip(jobs, sources):
        for k in range(last - first):
            place_one(plan, strip_ref, gap, metas[d], patch * total + first + k, source_ref[k])


def early_kernel(plan, jobs, total, *refs):
    metas, sources, strip_ref = refs[: plan.visits], refs[plan.visits : -1], refs[-1]
    strip_ref[...] = jnp.zeros_like(strip_ref)
    place_all(plan, strip_ref, total, metas, jobs, sources)


def early(plan, jobs, total, metas, sources):
    vmem = pl.BlockSpec(memory_space=pltpu.VMEM)
    shape = (plan.patches * plan.width // LANE + 2, plan.rows, LANE)
    return pl.pallas_call(
        functools.partial(early_kernel, plan, jobs, total),
        name="early",
        in_specs=[pl.BlockSpec(memory_space=pltpu.SMEM)] * plan.visits + [vmem] * len(sources),
        out_specs=vmem,
        out_shape=jax.ShapeDtypeStruct(shape, jnp.float32),
        compiler_params=pltpu.CompilerParams(vmem_limit_bytes=16 * MIB),
    )(*metas, *sources)


def late_kernel(plan, jobs, total, *refs):
    metas, rest = refs[: plan.visits], refs[plan.visits :]
    sources, rest = rest[: len(jobs)], rest[len(jobs) + 1 :]
    strip_ref, send_far, send_near, keep_far, keep_near = rest
    place_all(plan, strip_ref, total, metas, jobs, sources)

    rows, width = plan.rows, plan.width
    tiles = width // LANE
    patch = lax.axis_index("patch")
    core = patch & 1
    chip = patch >> 1
    pick = iota((8, LANE), 0) - 4
    lane = iota((8, LANE), 1)
    pick_left = ((pick >= 0) & (lane == LANE - 4 + pick)).astype(jnp.bfloat16)
    pick_right = ((pick >= 0) & (lane == pick)).astype(jnp.bfloat16)

    def across(table, block):
        out = lax.dot_general(table, block.astype(jnp.bfloat16), (((1,), (1,)), ((), ())), preferred_element_type=jnp.float32)
        return jnp.pad(out, ((0, 0), (0, LANE - rows)))

    def emit(m, parity, out_ref, spot):
        tile = (2 * (chip ^ m) + parity) * tiles + 1
        sides = (across(pick_left, strip_ref[tile - 1]), across(pick_right, strip_ref[tile + tiles]))
        for t in range(tiles):
            body = strip_ref[tile + t]
            if t < 2:
                body = jnp.concatenate([body[: rows - 8], body[rows - 8 :] + sides[t]], axis=0)
            out_ref[spot, :, t * LANE : (t + 1) * LANE] = body.astype(out_ref.dtype)

    near = plan.near
    for m in range(near, 2 * near):
        emit(m, 1 - core, send_far, m - near)
    for m in range(near):
        emit(m, 1 - core, send_near, m)
    for m in range(near, 2 * near):
        emit(m, core, keep_far, m - near)
    for m in range(near):
        emit(m, core, keep_near, m)


def late(plan, jobs, total, metas, sources, strip):
    vmem = pl.BlockSpec(memory_space=pltpu.VMEM)
    shape = (plan.near, plan.rows, plan.width)
    outs = [jax.ShapeDtypeStruct(strip.shape, strip.dtype)]
    outs += [jax.ShapeDtypeStruct(shape, jnp.bfloat16)] * 2 + [jax.ShapeDtypeStruct(shape, jnp.float32)] * 2
    return pl.pallas_call(
        functools.partial(late_kernel, plan, jobs, total),
        name="late",
        in_specs=[pl.BlockSpec(memory_space=pltpu.SMEM)] * plan.visits + [vmem] * (len(sources) + 1),
        out_specs=[vmem] * 5,
        out_shape=outs,
        input_output_aliases={plan.visits + len(sources): 0},
        compiler_params=pltpu.CompilerParams(vmem_limit_bytes=16 * MIB),
    )(*metas, *sources, strip)[1:]


def fold_kernel(keep_ref, got_ref, *outs):
    for m, out_ref in enumerate(outs):
        out_ref[...] = (keep_ref[m] + got_ref[m].astype(jnp.float32)).astype(out_ref.dtype)


def fold(plan, keep, got, own):
    vmem = pl.BlockSpec(memory_space=pltpu.VMEM)
    shape = (plan.rows, plan.width)
    types = [jnp.float32 if own and m == 0 else jnp.bfloat16 for m in range(plan.near)]
    return pl.pallas_call(
        fold_kernel,
        name="fold",
        in_specs=[vmem, vmem],
        out_specs=[vmem] * plan.near,
        out_shape=[jax.ShapeDtypeStruct(shape, dtype) for dtype in types],
        compiler_params=pltpu.CompilerParams(vmem_limit_bytes=6 * MIB),
    )(keep, got)


def cover_kernel(plan, *refs):
    metas, out_ref = refs[:-1], refs[-1]
    rows, width = plan.rows, plan.width
    column = lax.axis_index("patch") * width
    base = plan.base(lax.axis_index("visit"))
    total = jnp.zeros((LANE, width), jnp.float32)
    sides = jnp.zeros((LANE, LANE), jnp.float32)
    for meta_ref in metas:
        meta = meta_ref[...]
        count = meta.shape[0]
        local = iota((count, LANE), 1)
        sky = (local + base).astype(jnp.float32)
        oy = meta[:, 1:2]
        rho = jnp.where(sky >= oy, meta[:, 4:5], 0.0) + jnp.where(sky >= oy + 1.0, meta[:, 5:6], 0.0)
        rho = jnp.where((local < plan.useful) & (sky >= 0) & (sky < plan.height), meta[:, 6:7] * rho, 0.0)

        def kappa(place):
            gap = place.astype(jnp.float32) - meta[:, 0:1]
            return jnp.where((gap >= 0) & (gap < width), meta[:, 2:3], 0.0) + jnp.where(
                (gap >= 1) & (gap < width + 1), meta[:, 3:4], 0.0
            )

        spot = iota((count, LANE), 1)
        side = jnp.where(spot < 8, spot - 8, spot - 12 + width)
        known = ((spot >= 4) & (spot < 8)) | ((spot >= 12) & (spot < 16))
        edge = jnp.where(known, kappa(side + column), 0.0)
        dims = (((0,), (0,)), ((), ()))
        kinds = dict(preferred_element_type=jnp.float32, precision=lax.Precision.HIGHEST)
        total = total + lax.dot_general(rho, kappa(iota((count, width), 1) + column), dims, **kinds)
        sides = sides + lax.dot_general(edge, rho, dims, **kinds)
    tail = total[rows - 8 : rows]
    tail = jnp.concatenate([tail[:, :LANE] + sides[:8], tail[:, LANE : 2 * LANE] + sides[8:16], tail[:, 2 * LANE :]], axis=1)
    out_ref[...] = jnp.concatenate([total[: rows - 8], tail], axis=0)


def cover_of(plan, metas):
    vmem = pl.BlockSpec(memory_space=pltpu.VMEM)
    return pl.pallas_call(
        functools.partial(cover_kernel, plan),
        name="cover",
        in_specs=[vmem] * plan.visits,
        out_specs=vmem,
        out_shape=jax.ShapeDtypeStruct((plan.rows, plan.width), jnp.float32),
        compiler_params=pltpu.CompilerParams(vmem_limit_bytes=10 * MIB),
    )(*metas)


def finish_kernel(plan, filt, cover_ref, own_ref, *refs):
    parts, (coadd_ref, detect_ref) = refs[:-2], refs[-2:]
    rows, width, block = plan.rows, plan.width, plan.block
    flux = own_ref[...]
    for part in parts:
        flux = flux + part[...].astype(jnp.float32)
    coadd = flux / jnp.maximum(cover_ref[...], 1.0)
    visit = lax.axis_index("visit")
    if plan.step == block:
        coadd_ref[...] = coadd[-plan.first : -plan.first + block]
    else:
        coadd_ref[...] = jnp.where(visit == 0, coadd[:block], coadd[DRAD : DRAD + block])

    local = iota((block, LANE), 1)
    tap = local + plan.base(visit) - visit * block - iota((block, LANE), 0)
    good = (local < plan.useful) & (jnp.abs(tap) <= DRAD)
    band = jnp.zeros((block, LANE), jnp.float32)
    for t in range(-DRAD, DRAD + 1):
        band = jnp.where(good & (tap == t), filt[t + DRAD], band)
    kinds = dict(preferred_element_type=jnp.float32, precision=lax.Precision.HIGHEST)
    tall = jnp.concatenate([coadd, jnp.zeros((LANE - rows, width), jnp.float32)], axis=0)
    down = jnp.dot(band, tall, **kinds)
    blank = jnp.zeros((LANE - 8, LANE), jnp.float32)
    dims = (((1,), (1,)), ((), ()))
    before = lax.dot_general(band, jnp.concatenate([blank, coadd[rows - 8 :, :LANE]], axis=0), dims, **kinds)
    after = lax.dot_general(band, jnp.concatenate([coadd[rows - 8 :, LANE : 2 * LANE], blank], axis=0), dims, **kinds)
    lane = iota((block, LANE), 1)
    before = jnp.where(lane >= LANE - DRAD, before, 0.0)
    after = pltpu.roll(after, LANE - DRAD, 1)
    after = jnp.where(lane < DRAD, after, 0.0)
    wide = jnp.concatenate([before, down, after], axis=1)
    total = filt[DRAD] * wide
    for t in range(1, DRAD + 1):
        total = total + filt[DRAD + t] * (pltpu.roll(wide, t, 1) + pltpu.roll(wide, width + 2 * LANE - t, 1))
    detect_ref[...] = total[:, LANE : LANE + width]


def finish(plan, cover, own, parts):
    vmem = pl.BlockSpec(memory_space=pltpu.VMEM)
    t = np.arange(-DRAD, DRAD + 1).astype(np.float32)
    filt = np.exp(-t * t / np.float32(8.0))
    filt = filt / np.sqrt(np.sum(filt * filt))
    filt = [float(value) for value in filt]
    shape = jax.ShapeDtypeStruct((plan.block, plan.width), jnp.float32)
    return pl.pallas_call(
        functools.partial(finish_kernel, plan, filt),
        name="finish",
        in_specs=[vmem] * (2 + len(parts)),
        out_specs=[vmem, vmem],
        out_shape=[shape, shape],
        compiler_params=pltpu.CompilerParams(vmem_limit_bytes=10 * MIB),
    )(cover, own, *parts)


def narrow(value):
    return lax.reduce_precision(value, 8, 7)


def local(mesh, images, coefficients, intersection, row_offset, col_offset, shifts, inv_var):
    count, height, width = images.shape[1:]
    plan = Plan(mesh, height, width)
    taps = basis_taps()
    table, rows = jnp.asarray(column_table(taps)), jnp.asarray(row_table(taps))
    frac_row, frac_col = shifts[0, :, 0:1], shifts[0, :, 1:2]
    start = intersection[0, :, 0:1] * width + col_offset[0][:, None]
    meta = jnp.concatenate(
        [
            start.astype(jnp.float32),
            row_offset[0][:, None].astype(jnp.float32),
            narrow(1.0 - frac_col),
            narrow(frac_col),
            narrow(1.0 - frac_row),
            narrow(frac_row),
            inv_var[0][:, None],
            jnp.zeros_like(frac_row),
        ],
        axis=1,
    )

    sides, factors = jnp.transpose(shifts, (0, 2, 1)), jnp.transpose(coefficients, (1, 2, 0, 3))

    def swap(value, axis, bit):
        return lax.ppermute(value, axis, [(i, i ^ bit) for i in range(mesh.shape[axis])])

    metas = [meta] + [swap(meta, "visit", d) for d in range(1, plan.visits)]
    chunks = [(lo, min(hi, count)) for lo, hi in CHUNKS]
    ready, last = [], []
    for n, (lo, hi) in enumerate(chunks):
        slots = match(plan, (lo, hi), True, row_offset, sides, factors, images, table, rows)
        ready.append(((0, lo, hi), slots[0]))
        group = last if n == len(chunks) - 1 else ready
        group += [((d, lo, hi), swap(slots[d], "visit", d)) for d in range(1, plan.visits)]
    strip = early(plan, [job for job, _ in ready], count, metas, [source for _, source in ready])
    send_far, send_near, keep_far, keep_near = late(plan, [job for job, _ in last], count, metas, [source for _, source in last], strip)
    cover = cover_of(plan, metas)
    far = fold(plan, keep_far, swap(send_far, "patch", 1), False)
    near = fold(plan, keep_near, swap(send_near, "patch", 1), True)
    folded = list(near) + list(far)
    parts = [swap(folded[m], "patch", 2 * m) for m in range(2 * plan.near - 1, 0, -1)]
    return finish(plan, cover, near[0], parts)


def solution(mesh):
    return jax.shard_map(
        functools.partial(local, mesh),
        mesh=mesh,
        in_specs=(
            P("visit", "patch", None, None),
            P("visit", "patch", None, None),
            P("visit", None, None),
            P("visit", None),
            P("visit", None),
            P("visit", None, None),
            P("visit", None),
        ),
        out_specs=(P("visit", "patch"), P("visit", "patch")),
        check_vma=False,
    )
```
